32 devices in a mesh: row: 16 (over z, y, x), col: 2 (over core).
Axes of the slice: x: 2, y: 2, z: 4, core: 2. Of those that a mesh axis runs over, the one named last changes fastest.
Arguments:
- kernel: float32 [1024, 65536], P('row', 'col'), may hold values from -6 to 6
- basis: float32 [65536, 128], P('col', 'row'), may hold values from -0.0234375 to 0.0234375
- responses: float32 [1024, 512], P('row', 'col'), may hold values from -6 to 6
Outputs:
- scores: float32 [1024, 128], P('row')
- loadings: float32 [128, 65536], P('row', 'col')
- weights: float32 [512, 128], P('col')
- deflated: float32 [1024, 65536], P('row', 'col')
- basis_next: float32 [1024, 128], P('row')
The draws below stay inside these ranges and needn't reach their ends.
All inputs are finite; a program needn't handle non-finite values.
Results may differ from the reference program's by a relative error of at most 0.00012.
Values sent between devices are 32-bit elements; how exact they have to be, the bound alone decides.
A program may use at most 64 MiB of HBM per device.

```python
import math
import jax
import jax.numpy as jnp
from jax import lax

N = 65536
COMP = 128
M = 512
ROWS = 1024


def steps_of(own_key, dims, pieces, least, high):
    gain = 1.0
    for dim, blocks in pieces:
        steps = jax.random.uniform(jax.random.fold_in(jax.random.fold_in(own_key, 6), dim), (blocks,), jnp.float32, least / len(pieces), high / len(pieces))
        gain = gain * jnp.repeat(jnp.exp(steps), dims[dim] // blocks).reshape((-1,) + (1,) * (len(dims) - 1 - dim))
    return gain


def centred(key, dims, spread, limit, split=(), held_as=jnp.bfloat16):
    loudness = steps_of(key, dims, split, -0.22, 0.18) if split else 1.0
    result = jax.random.normal(key, dims, jnp.float32) * spread * loudness
    return jnp.minimum(jnp.maximum(result, -limit), limit).astype(held_as)


def setup_inputs(seed: int = 0) -> dict:
    key_of = jax.random.split(jax.random.key(seed), 4)
    kernel = centred(key_of[0], (ROWS, N), 1.0, 6.0, ((0, 16), (1, 2)), jnp.float32)
    basis = centred(key_of[1], (N, COMP), N ** -0.5, 0.0234375, ((0, 2), (1, 16)), jnp.float32)
    responses = centred(key_of[2], (ROWS, M), 1.0, 6.0, ((0, 16), (1, 2)), jnp.float32)
    return dict(kernel=kernel, basis=basis, responses=responses)


def reference(kernel, basis, responses):
    highest = lax.Precision.HIGHEST
    root_rows = math.sqrt(ROWS)
    projected = jnp.dot(kernel, basis, precision=highest)
    gram_mat = jnp.dot(projected.T, projected, precision=highest) / ROWS
    factor = jnp.linalg.cholesky(gram_mat)
    scores = jax.scipy.linalg.solve_triangular(factor, projected.T, lower=True).T
    loadings = jnp.dot(scores.T, kernel, precision=highest) / root_rows
    deflated = kernel - jnp.dot(scores, loadings, precision=highest) / root_rows
    weights = jnp.dot(responses.T, scores, precision=highest) / root_rows
    basis_next = jnp.dot(responses, weights, precision=highest) / math.sqrt(M)
    return (scores, loadings, weights, deflated, basis_next)
```

```python
import math

import jax
import jax.numpy as jnp
from jax import lax
from jax.experimental import pallas as pl
from jax.experimental.pallas import tpu as pltpu
from jax.sharding import PartitionSpec as P

MESH = pl.DeviceIdType.MESH
BACK = {"x": "x", "y": "y", "up": "down", "down": "up"}


def when(conds):
    conds = [c for c in conds if c is not None]
    if not conds:
        return lambda f: f()
    both = conds[0]
    for c in conds[1:]:
        both = jnp.logical_and(both, c)
    return pl.when(both)


class Grid:
    def __init__(self, n):
        self.n = n
        self.size = {"z": n // 4, "y": 2, "x": 2} if n % 4 == 0 else {"z": n, "y": 1, "x": 1}
        z = self.size["z"]
        self.rels = [
            (dz, fy, fx)
            for dz in range(1 - z, z)
            for fy in range(self.size["y"])
            for fx in range(self.size["x"])
        ]
        self.rels.sort(key=lambda r: (abs(r[0]) + r[1] + r[2], -abs(r[0])))

    def locate(self):
        me = lax.axis_index("row")
        ny, nx = self.size["y"], self.size["x"]
        self.me = me
        self.z = me // (ny * nx)
        self.y = (me // nx) % ny
        self.x = me % nx

    def coords(self, rel):
        dz, fy, fx = rel
        return {
            "z": self.z + dz,
            "y": 1 - self.y if fy else self.y,
            "x": 1 - self.x if fx else self.x,
        }

    def index(self, rel):
        c = self.coords(rel)
        return (c["z"] * self.size["y"] + c["y"]) * self.size["x"] + c["x"]

    def valid(self, rel):
        dz = rel[0]
        if dz == 0:
            return None
        return self.z < self.size["z"] - dz if dz > 0 else self.z >= -dz

    def neighbour(self, link):
        rel = {"x": (0, 0, 1), "y": (0, 1, 0), "up": (1, 0, 0), "down": (-1, 0, 0)}[link]
        return self.index(rel)

    def has(self, link):
        if link == "up":
            return self.z < self.size["z"] - 1
        if link == "down":
            return self.z > 0
        return None

    def links(self):
        found = [d for d in "xy" if self.size[d] > 1]
        return found + (["up", "down"] if self.size["z"] > 1 else [])

    def last(self, order, rel):
        differs = {"z": rel[0] != 0, "y": rel[1] != 0, "x": rel[2] != 0}
        found = [k for k, d in enumerate(order) if differs[d]]
        return found[-1] if found else -1

    def away(self, order, rel):
        k = self.last(order, rel)
        found = []
        for j, d in enumerate(order):
            if j < k or self.size[d] == 1:
                continue
            if d != "z":
                found += [d] if j > k else []
            elif j > k:
                found += ["up", "down"]
            else:
                found += ["down" if rel[0] > 0 else "up"]
        return found

    def towards(self, order, rel):
        d = order[self.last(order, rel)]
        if d != "z":
            return d
        return "up" if rel[0] > 0 else "down"

    def slot_dims(self, order, link):
        if link in "xy":
            return order[: order.index(link)]
        return order[: order.index("z") + 1]

    def slots(self, order, link):
        return math.prod(self.size[d] for d in self.slot_dims(order, link))

    def slot(self, order, link, rel):
        c = self.coords(rel)
        at = 0
        for d in self.slot_dims(order, link):
            at = at * self.size[d] + c[d]
        return at

    def barrier(self):
        barrier = pltpu.get_barrier_semaphore()
        count = 0
        for link in self.links():
            cond = self.has(link)

            @when([cond])
            def _(link=link):
                pl.semaphore_signal(
                    barrier, inc=1, device_id={"row": self.neighbour(link)}, device_id_type=MESH
                )

            count = count + (1 if cond is None else cond.astype(jnp.int32))
        pl.semaphore_wait(barrier, count)


def parts_of(width):
    tile = 128
    tiles = width // tile
    thin = tiles // 9
    if thin == 0:
        return [(0, width, "zyx")]
    wide = [(tiles - 2 * thin + 3 - i) // 4 for i in range(4)]
    pieces = [
        (wide[0], "zyx"),
        (wide[1], "zxy"),
        (thin, "xyz"),
        (thin, "yxz"),
        (wide[2], "zyx"),
        (wide[3], "zxy"),
    ]
    found, start = [], 0
    for count, order in pieces:
        if count:
            found.append((start * tile, count * tile, order))
            start += count
    return found


def sem_shapes(grid, orders):
    return [
        [pltpu.SemaphoreType.DMA((grid.slots(order, link),)) for link in grid.links()]
        for order in orders
    ]


def gather_start(grid, rel, part, order, src, dst, send, recv):
    row = grid.index(rel)
    for link in grid.away(order, rel):

        @when([grid.valid(rel), grid.has(link)])
        def _(link=link):
            gather_copy(grid, rel, part, order, link, src(row), dst(row), send, recv).start()


def gather_copy(grid, rel, part, order, link, src, dst, send, recv):
    return pltpu.make_async_remote_copy(
        src_ref=src,
        dst_ref=dst,
        send_sem=send[part][grid.links().index(link)].at[grid.slot(order, link, rel)],
        recv_sem=recv.at[part, grid.index(rel)],
        device_id={"row": grid.neighbour(link)},
        device_id_type=MESH,
    )


def gather_finish(grid, parts, dst, send, recv):
    for rel in grid.rels[1:]:
        for part, order in parts:

            @when([grid.valid(rel)])
            def _(rel=rel, part=part, order=order):
                row = grid.index(rel)
                pltpu.make_async_copy(dst(part, row), dst(part, row), recv.at[part, row]).wait()

            gather_start(
                grid, rel, part, order, lambda r: dst(part, r), lambda r: dst(part, r), send, recv
            )
    for rel in grid.rels:
        for part, order in parts:
            for link in grid.away(order, rel):

                @when([grid.valid(rel), grid.has(link)])
                def _(rel=rel, part=part, order=order, link=link):
                    ref = dst(part, grid.index(rel))
                    gather_copy(grid, rel, part, order, link, ref, ref, send, recv).wait_send()


def all_gather(block, collective_id):
    n = lax.axis_size("row")
    grid = Grid(n)
    parts = parts_of(block.shape[1]) if block.shape[1] >= 1152 else [(0, block.shape[1], "zyx")]
    numbered = [(i, order) for i, (_, _, order) in enumerate(parts)]

    def kernel(own, out, own_sem, recv, send):
        grid.locate()
        keep = pltpu.make_async_copy(own, out.at[grid.me], own_sem)
        keep.start()
        grid.barrier()

        def dst(part, row):
            start, width, _ = parts[part]
            return out.at[row, :, pl.ds(start, width)]

        for part, order in numbered:
            start, width, _ = parts[part]
            gather_start(
                grid,
                (0, 0, 0),
                part,
                order,
                lambda r: own.at[:, pl.ds(start, width)],
                lambda r: dst(part, r),
                send,
                recv,
            )
        gather_finish(grid, numbered, dst, send, recv)
        keep.wait()

    return pl.pallas_call(
        kernel,
        out_shape=jax.ShapeDtypeStruct((n, *block.shape), block.dtype),
        in_specs=[pl.BlockSpec(memory_space=pl.ANY)],
        out_specs=pl.BlockSpec(memory_space=pl.ANY),
        scratch_shapes=[
            pltpu.SemaphoreType.DMA,
            pltpu.SemaphoreType.DMA((len(parts), n)),
            sem_shapes(grid, [o for _, _, o in parts]),
        ],
        compiler_params=pltpu.CompilerParams(collective_id=collective_id, has_side_effects=True),
    )(block)


def all_reduce(arrays, collective_id):
    n = lax.axis_size("row")
    grid = Grid(n)
    parts = [(i, *p) for i, a in enumerate(arrays) for p in parts_of(a.shape[2])]
    parts.sort(key=lambda p: -p[0])
    orders = [p[3] for p in parts]
    numbered = list(enumerate(orders))
    count = len(arrays)

    def kernel(*refs):
        sources, outs, held = refs[:count], refs[count : 2 * count], refs[2 * count : 3 * count]
        inbox, load_sem, keep_sem, sum_send, sum_recv, send, recv = refs[3 * count :]
        grid.locate()

        def load(i, row):
            return pltpu.make_async_copy(sources[i].at[row], held[i].at[row], load_sem.at[i, row])

        for rel in reversed(grid.rels):
            for i in range(count):

                @when([grid.valid(rel)])
                def _(rel=rel, i=i):
                    load(i, grid.index(rel)).start()

        grid.barrier()

        def kept(part, row):
            i, start, width, _ = parts[part]
            return held[i].at[row, :, pl.ds(start, width)]

        def dst(part, row):
            i, start, width, _ = parts[part]
            return outs[i].at[row, :, pl.ds(start, width)]

        def sum_copy(rel, part, order):
            link = grid.towards(order, rel)
            at = grid.slot(order, BACK[link], rel)
            there = grid.links().index(BACK[link])
            row = grid.index(rel)
            return pltpu.make_async_remote_copy(
                src_ref=kept(part, row),
                dst_ref=inbox[part][there].at[at],
                send_sem=sum_send.at[part, row],
                recv_sem=sum_recv[part][there].at[at],
                device_id={"row": grid.neighbour(link)},
                device_id_type=MESH,
            )

        for rel in reversed(grid.rels):
            for i in range(count):

                @when([grid.valid(rel)])
                def _(rel=rel, i=i):
                    load(i, grid.index(rel)).wait()

            for part, order in numbered:
                i, start, width, _ = parts[part]
                for link in grid.away(order, rel):

                    @when([grid.valid(rel), grid.has(link)])
                    def _(rel=rel, part=part, order=order, link=link):
                        row, at = grid.index(rel), grid.slot(order, link, rel)
                        here = grid.links().index(link)
                        slot = inbox[part][here].at[at]
                        pltpu.make_async_copy(slot, slot, sum_recv[part][here].at[at]).wait()
                        columns = pl.ds(start, width)
                        held[i][row, :, columns] = held[i][row, :, columns] + inbox[part][here][at]

                if rel != (0, 0, 0):

                    @when([grid.valid(rel)])
                    def _(rel=rel, part=part, order=order):
                        sum_copy(rel, part, order).start()

                else:
                    pltpu.make_async_copy(
                        kept(part, grid.me), dst(part, grid.me), keep_sem.at[part]
                    ).start()
                    gather_start(
                        grid,
                        rel,
                        part,
                        order,
                        lambda r: kept(part, r),
                        lambda r: dst(part, r),
                        send,
                        recv,
                    )
        gather_finish(grid, numbered, dst, send, recv)
        for rel in grid.rels:
            for part, order in numbered:
                if rel != (0, 0, 0):

                    @when([grid.valid(rel)])
                    def _(rel=rel, part=part, order=order):
                        sum_copy(rel, part, order).wait_send()

                else:
                    pltpu.make_async_copy(
                        kept(part, grid.me), dst(part, grid.me), keep_sem.at[part]
                    ).wait()

    return pl.pallas_call(
        kernel,
        out_shape=[jax.ShapeDtypeStruct(a.shape, a.dtype) for a in arrays],
        in_specs=[pl.BlockSpec(memory_space=pl.ANY)] * count,
        out_specs=[pl.BlockSpec(memory_space=pl.ANY)] * count,
        scratch_shapes=[
            *[pltpu.VMEM(a.shape, a.dtype) for a in arrays],
            [
                [
                    pltpu.VMEM((grid.slots(order, link), arrays[i].shape[1], width), jnp.float32)
                    for link in grid.links()
                ]
                for i, _, width, order in parts
            ],
            pltpu.SemaphoreType.DMA((count, n)),
            pltpu.SemaphoreType.DMA((len(parts),)),
            pltpu.SemaphoreType.DMA((len(parts), n)),
            sem_shapes(grid, orders),
            sem_shapes(grid, orders),
            pltpu.SemaphoreType.DMA((len(parts), n)),
        ],
        compiler_params=pltpu.CompilerParams(
            collective_id=collective_id, has_side_effects=True, vmem_limit_bytes=60 * 2**20
        ),
    )(*arrays)


def local(kernel, basis, responses):
    highest = lax.Precision.HIGHEST
    n = lax.axis_size("row")
    row_count = kernel.shape[0] * n
    resp_count = responses.shape[1] * lax.axis_size("col")
    comp = basis.shape[1] * n
    root_rows = math.sqrt(row_count)
    last_dims = (((1,), (1,)), ((), ()))
    first_dims = (((0,), (0,)), ((), ()))

    all_basis = all_gather(basis.T, 0).reshape(comp, basis.shape[0])
    partial_proj = lax.dot_general(kernel, all_basis, last_dims, precision=highest)
    projected = lax.psum(partial_proj, "col")
    all_projected = all_gather(projected, 1).reshape(row_count, comp)
    gram_mat = lax.dot_general(all_projected, all_projected, first_dims, precision=highest)
    factor = jnp.linalg.cholesky(gram_mat / row_count)
    scores = jax.scipy.linalg.solve_triangular(factor, projected.T, lower=True).T

    load_part = lax.dot_general(scores, kernel, first_dims, precision=highest) / root_rows
    weight_part = lax.dot_general(responses, scores, first_dims, precision=highest) / root_rows
    all_loadings, all_weights = all_reduce(
        [
            load_part.reshape(n, comp // n, kernel.shape[1]),
            weight_part.reshape(n, responses.shape[1] // n, comp),
        ],
        2,
    )
    loadings = lax.dynamic_index_in_dim(all_loadings, lax.axis_index("row"), keepdims=False)
    weights = all_weights.reshape(responses.shape[1], comp)
    next_part = jnp.dot(responses, weights, precision=highest) / math.sqrt(resp_count)
    basis_next = lax.psum(next_part, "col")
    all_loadings = all_loadings.reshape(comp, kernel.shape[1])
    deflated = kernel - jnp.dot(scores, all_loadings, precision=highest) / root_rows
    return (scores, loadings, weights, deflated, basis_next)


def solution(mesh):
    return jax.shard_map(
        local,
        mesh=mesh,
        in_specs=(P("row", "col"), P("col", "row"), P("row", "col")),
        out_specs=(
            P("row", None),
            P("row", "col"),
            P("col", None),
            P("row", "col"),
            P("row", None),
        ),
        check_vma=False,
    )
```

```python
import math

import jax
import jax.numpy as jnp
from jax import lax
from jax.experimental import pallas as pl
from jax.experimental.pallas import tpu as pltpu
from jax.sharding import PartitionSpec as P

MESH = pl.DeviceIdType.MESH
BACK = {"x": "x", "y": "y", "up": "down", "down": "up"}


def when(conds):
    conds = [c for c in conds if c is not None]
    if not conds:
        return lambda f: f()
    both = conds[0]
    for c in conds[1:]:
        both = jnp.logical_and(both, c)
    return pl.when(both)


class Grid:
    def __init__(self, n):
        self.n = n
        self.size = {"z": n // 4, "y": 2, "x": 2} if n % 4 == 0 else {"z": n, "y": 1, "x": 1}
        z = self.size["z"]
        self.rels = [
            (dz, fy, fx)
            for dz in range(1 - z, z)
            for fy in range(self.size["y"])
            for fx in range(self.size["x"])
        ]
        self.rels.sort(key=lambda r: (abs(r[0]) + r[1] + r[2], -abs(r[0])))

    def locate(self):
        me = lax.axis_index("row")
        ny, nx = self.size["y"], self.size["x"]
        self.me = me
        self.z = me // (ny * nx)
        self.y = (me // nx) % ny
        self.x = me % nx

    def coords(self, rel):
        dz, fy, fx = rel
        return {
            "z": self.z + dz,
            "y": 1 - self.y if fy else self.y,
            "x": 1 - self.x if fx else self.x,
        }

    def index(self, rel):
        c = self.coords(rel)
        return (c["z"] * self.size["y"] + c["y"]) * self.size["x"] + c["x"]

    def valid(self, rel):
        dz = rel[0]
        if dz == 0:
            return None
        return self.z < self.size["z"] - dz if dz > 0 else self.z >= -dz

    def neighbour(self, link):
        rel = {"x": (0, 0, 1), "y": (0, 1, 0), "up": (1, 0, 0), "down": (-1, 0, 0)}[link]
        return self.index(rel)

    def has(self, link):
        if link == "up":
            return self.z < self.size["z"] - 1
        if link == "down":
            return self.z > 0
        return None

    def links(self):
        found = [d for d in "xy" if self.size[d] > 1]
        return found + (["up", "down"] if self.size["z"] > 1 else [])

    def last(self, order, rel):
        differs = {"z": rel[0] != 0, "y": rel[1] != 0, "x": rel[2] != 0}
        found = [k for k, d in enumerate(order) if differs[d]]
        return found[-1] if found else -1

    def away(self, order, rel):
        k = self.last(order, rel)
        found = []
        for j, d in enumerate(order):
            if j < k or self.size[d] == 1:
                continue
            if d != "z":
                found += [d] if j > k else []
            elif j > k:
                found += ["up", "down"]
            else:
                found += ["down" if rel[0] > 0 else "up"]
        return found

    def towards(self, order, rel):
        d = order[self.last(order, rel)]
        if d != "z":
            return d
        return "up" if rel[0] > 0 else "down"

    def slot_dims(self, order, link):
        if link in "xy":
            return order[: order.index(link)]
        return order[: order.index("z") + 1]

    def slots(self, order, link):
        return math.prod(self.size[d] for d in self.slot_dims(order, link))

    def slot(self, order, link, rel):
        c = self.coords(rel)
        at = 0
        for d in self.slot_dims(order, link):
            at = at * self.size[d] + c[d]
        return at

    def barrier(self):
        barrier = pltpu.get_barrier_semaphore()
        count = 0
        for link in self.links():
            cond = self.has(link)

            @when([cond])
            def _(link=link):
                pl.semaphore_signal(
                    barrier, inc=1, device_id={"row": self.neighbour(link)}, device_id_type=MESH
                )

            count = count + (1 if cond is None else cond.astype(jnp.int32))
        pl.semaphore_wait(barrier, count)


def parts_of(width):
    tile = 128
    tiles = width // tile
    thin = tiles // 9
    if thin == 0:
        return [(0, width, "zyx")]
    wide = [(tiles - 2 * thin + 3 - i) // 4 for i in range(4)]
    pieces = [
        (wide[0], "zyx"),
        (wide[1], "zxy"),
        (thin, "xyz"),
        (thin, "yxz"),
        (wide[2], "zyx"),
        (wide[3], "zxy"),
    ]
    found, start = [], 0
    for count, order in pieces:
        if count:
            found.append((start * tile, count * tile, order))
            start += count
    return found


def sem_shapes(grid, orders):
    return [
        [pltpu.SemaphoreType.DMA((grid.slots(order, link),)) for link in grid.links()]
        for order in orders
    ]


def gather_start(grid, rel, part, order, src, dst, send, recv):
    row = grid.index(rel)
    for link in grid.away(order, rel):

        @when([grid.valid(rel), grid.has(link)])
        def _(link=link):
            gather_copy(grid, rel, part, order, link, src(row), dst(row), send, recv).start()


def gather_copy(grid, rel, part, order, link, src, dst, send, recv):
    return pltpu.make_async_remote_copy(
        src_ref=src,
        dst_ref=dst,
        send_sem=send[part][grid.links().index(link)].at[grid.slot(order, link, rel)],
        recv_sem=recv.at[part, grid.index(rel)],
        device_id={"row": grid.neighbour(link)},
        device_id_type=MESH,
    )


def gather_finish(grid, parts, dst, send, recv):
    for rel in grid.rels[1:]:
        for part, order in parts:

            @when([grid.valid(rel)])
            def _(rel=rel, part=part, order=order):
                row = grid.index(rel)
                pltpu.make_async_copy(dst(part, row), dst(part, row), recv.at[part, row]).wait()

            gather_start(
                grid, rel, part, order, lambda r: dst(part, r), lambda r: dst(part, r), send, recv
            )
    for rel in grid.rels:
        for part, order in parts:
            for link in grid.away(order, rel):

                @when([grid.valid(rel), grid.has(link)])
                def _(rel=rel, part=part, order=order, link=link):
                    ref = dst(part, grid.index(rel))
                    gather_copy(grid, rel, part, order, link, ref, ref, send, recv).wait_send()


def all_gather(block, collective_id):
    n = lax.axis_size("row")
    grid = Grid(n)
    parts = parts_of(block.shape[1]) if block.shape[1] >= 1152 else [(0, block.shape[1], "zyx")]
    numbered = [(i, order) for i, (_, _, order) in enumerate(parts)]

    def kernel(own, out, own_sem, recv, send):
        grid.locate()
        keep = pltpu.make_async_copy(own, out.at[grid.me], own_sem)
        keep.start()
        grid.barrier()

        def dst(part, row):
            start, width, _ = parts[part]
            return out.at[row, :, pl.ds(start, width)]

        for part, order in numbered:
            start, width, _ = parts[part]
            gather_start(
                grid,
                (0, 0, 0),
                part,
                order,
                lambda r: own.at[:, pl.ds(start, width)],
                lambda r: dst(part, r),
                send,
                recv,
            )
        gather_finish(grid, numbered, dst, send, recv)
        keep.wait()

    return pl.pallas_call(
        kernel,
        out_shape=jax.ShapeDtypeStruct((n, *block.shape), block.dtype),
        in_specs=[pl.BlockSpec(memory_space=pl.ANY)],
        out_specs=pl.BlockSpec(memory_space=pl.ANY),
        scratch_shapes=[
            pltpu.SemaphoreType.DMA,
            pltpu.SemaphoreType.DMA((len(parts), n)),
            sem_shapes(grid, [o for _, _, o in parts]),
        ],
        compiler_params=pltpu.CompilerParams(collective_id=collective_id, has_side_effects=True),
    )(block)


def tile_of(width, limit):
    return max([t for t in range(128, limit + 1, 128) if width % t == 0], default=width)


def cross_sums(kernel_rows, rows_t, small, collective_id):
    n = lax.axis_size("row")
    grid = Grid(n)
    height, total = kernel_rows.shape
    block = rows_t.shape[0] // n
    shapes = [(n, block, total), small.shape]
    parts = [(i, *p) for i, shape in enumerate(shapes) for p in parts_of(shape[2])]
    parts.sort(key=lambda p: (-p[0], p[3][0] == "z", p[1]))
    orders = [p[3] for p in parts]
    numbered = list(enumerate(orders))

    def body(
        kernel_ref,
        rows_ref,
        small_ref,
        out,
        small_out,
        held_big,
        held_small,
        kernel_held,
        inbox,
        load_sem,
        small_sem,
        keep_sem,
        sum_send,
        sum_recv,
        send,
        recv,
    ):
        held, outs = (held_big, held_small), (out, small_out)
        grid.locate()

        def load(part):
            _, start, width, _ = parts[part]
            columns = pl.ds(start, width)
            return pltpu.make_async_copy(
                kernel_ref.at[:, columns], kernel_held.at[:, columns], load_sem.at[part]
            )

        load_small = pltpu.make_async_copy(small_ref, held_small, small_sem)
        load_small.start()
        for part, (i, _, _, _) in enumerate(parts):
            if i == 0:
                load(part).start()
        grid.barrier()

        def kept(part, row):
            i, start, width, _ = parts[part]
            return held[i].at[row, :, pl.ds(start, width)]

        def dst(part, row):
            i, start, width, _ = parts[part]
            return outs[i].at[row, :, pl.ds(start, width)]

        def sum_copy(rel, part, order):
            link = grid.towards(order, rel)
            at = grid.slot(order, BACK[link], rel)
            there = grid.links().index(BACK[link])
            row = grid.index(rel)
            return pltpu.make_async_remote_copy(
                src_ref=kept(part, row),
                dst_ref=inbox[part][there].at[at],
                send_sem=sum_send.at[part, row],
                recv_sem=sum_recv[part][there].at[at],
                device_id={"row": grid.neighbour(link)},
                device_id_type=MESH,
            )

        def pass_on(rel, part, order):
            @when([grid.valid(rel)])
            def _():
                sum_copy(rel, part, order).start()

        for part, order in numbered:
            i, start, width, _ = parts[part]
            if i == 0:
                load(part).wait()
                tile = tile_of(width, 1280)

                @pl.loop(0, width // tile)
                def _(step, start=start, tile=tile):
                    columns = pl.ds(pl.multiple_of(start + step * tile, 128), tile)
                    product = jnp.dot(
                        rows_ref[...],
                        kernel_held[:, columns],
                        precision=lax.Precision.HIGHEST,
                        preferred_element_type=jnp.float32,
                    )
                    for row in range(n):
                        held_big[row, :, columns] = product[row * block : (row + 1) * block]

            else:
                load_small.wait()
            for rel in reversed(grid.rels[1:]):
                if not grid.away(order, rel):
                    pass_on(rel, part, order)

        for rel in reversed(grid.rels):
            for part, order in numbered:
                i, start, width, _ = parts[part]
                links = grid.away(order, rel)
                for link in links:

                    @when([grid.valid(rel), grid.has(link)])
                    def _(rel=rel, part=part, order=order, link=link):
                        row, at = grid.index(rel), grid.slot(order, link, rel)
                        here = grid.links().index(link)
                        slot = inbox[part][here].at[at]
                        pltpu.make_async_copy(slot, slot, sum_recv[part][here].at[at]).wait()
                        columns = pl.ds(start, width)
                        held[i][row, :, columns] = held[i][row, :, columns] + inbox[part][here][at]

                if rel != (0, 0, 0):
                    if links:
                        pass_on(rel, part, order)
                else:
                    pltpu.make_async_copy(
                        kept(part, grid.me), dst(part, grid.me), keep_sem.at[part]
                    ).start()
                    gather_start(
                        grid,
                        rel,
                        part,
                        order,
                        lambda r: kept(part, r),
                        lambda r: dst(part, r),
                        send,
                        recv,
                    )
        gather_finish(grid, numbered, dst, send, recv)
        for rel in grid.rels:
            for part, order in numbered:
                if rel != (0, 0, 0):

                    @when([grid.valid(rel)])
                    def _(rel=rel, part=part, order=order):
                        sum_copy(rel, part, order).wait_send()

                else:
                    pltpu.make_async_copy(
                        kept(part, grid.me), dst(part, grid.me), keep_sem.at[part]
                    ).wait()

    return pl.pallas_call(
        body,
        out_shape=[jax.ShapeDtypeStruct(shape, jnp.float32) for shape in shapes],
        in_specs=[
            pl.BlockSpec(memory_space=pl.ANY),
            pl.BlockSpec(memory_space=pltpu.VMEM),
            pl.BlockSpec(memory_space=pl.ANY),
        ],
        out_specs=[pl.BlockSpec(memory_space=pl.ANY)] * 2,
        scratch_shapes=[
            *[pltpu.VMEM(shape, jnp.float32) for shape in shapes],
            pltpu.VMEM((height, total), jnp.float32),
            [
                [
                    pltpu.VMEM((grid.slots(order, link), shapes[i][1], width), jnp.float32)
                    for link in grid.links()
                ]
                for i, _, width, order in parts
            ],
            pltpu.SemaphoreType.DMA((len(parts),)),
            pltpu.SemaphoreType.DMA,
            pltpu.SemaphoreType.DMA((len(parts),)),
            pltpu.SemaphoreType.DMA((len(parts), n)),
            sem_shapes(grid, orders),
            sem_shapes(grid, orders),
            pltpu.SemaphoreType.DMA((len(parts), n)),
        ],
        compiler_params=pltpu.CompilerParams(
            collective_id=collective_id, has_side_effects=True, vmem_limit_bytes=60 * 2**20
        ),
    )(kernel_rows, rows_t, small)


def deflate(kernel_rows, sums, rows, own):
    height, total = kernel_rows.shape
    comp = sums.shape[0]
    tile = tile_of(total, 2048)

    def body(kernel_ref, sums_ref, rows_ref, own_ref, deflated_ref, own_out):
        def times(left):
            return jnp.dot(
                left[...],
                sums_ref[...],
                precision=lax.Precision.HIGHEST,
                preferred_element_type=jnp.float32,
            )

        deflated_ref[...] = kernel_ref[...] - times(rows_ref)
        own_out[...] = times(own_ref)

    def columns(size):
        return pl.BlockSpec((size, tile), lambda i: (0, i))

    return pl.pallas_call(
        body,
        grid=(total // tile,),
        out_shape=[
            jax.ShapeDtypeStruct(kernel_rows.shape, jnp.float32),
            jax.ShapeDtypeStruct((own.shape[0], total), jnp.float32),
        ],
        in_specs=[
            columns(height),
            columns(comp),
            pl.BlockSpec(rows.shape, lambda i: (0, 0)),
            pl.BlockSpec(own.shape, lambda i: (0, 0)),
        ],
        out_specs=[columns(height), columns(own.shape[0])],
    )(kernel_rows, sums, rows, own)


def local(kernel, basis, responses):
    highest = lax.Precision.HIGHEST
    n = lax.axis_size("row")
    height, total = kernel.shape
    responses_here = responses.shape[1]
    row_count = height * n
    resp_count = responses_here * lax.axis_size("col")
    comp = basis.shape[1] * n
    root_rows = math.sqrt(row_count)
    last_dims = (((1,), (1,)), ((), ()))
    first_dims = (((0,), (0,)), ((), ()))

    all_basis = all_gather(basis.T, 0).reshape(comp, total)
    partial_proj = lax.dot_general(kernel, all_basis, last_dims, precision=highest)
    projected = lax.psum(partial_proj, "col")

    small_part = lax.dot_general(
        jnp.concatenate([responses, projected], axis=1), projected, first_dims, precision=highest
    )
    sums, small = cross_sums(
        kernel, projected.T, small_part.reshape(n, (responses_here + comp) // n, comp), 1
    )
    small = small.reshape(responses_here + comp, comp)
    factor = jnp.linalg.cholesky(small[responses_here:] / row_count)
    right = jnp.concatenate(
        [projected.T, small[:responses_here].T, jnp.eye(comp, dtype=jnp.float32)], axis=1
    )
    solved = jax.scipy.linalg.solve_triangular(factor, right, lower=True)
    scores = solved[:, :height].T
    weights = solved[:, height : height + responses_here].T / root_rows
    inverse = solved[:, height + responses_here :] / root_rows
    next_part = jnp.dot(responses, weights, precision=highest) / math.sqrt(resp_count)
    basis_next = lax.psum(next_part, "col")
    deflated, loadings = deflate(
        kernel,
        sums.reshape(comp, total),
        jnp.dot(scores, inverse, precision=highest) / root_rows,
        lax.dynamic_slice_in_dim(inverse, lax.axis_index("row") * (comp // n), comp // n),
    )
    return (scores, loadings, weights, deflated, basis_next)


def solution(mesh):
    return jax.shard_map(
        local,
        mesh=mesh,
        in_specs=(P("row", "col"), P("col", "row"), P("row", "col")),
        out_specs=(
            P("row", None),
            P("row", "col"),
            P("col", None),
            P("row", "col"),
            P("row", None),
        ),
        check_vma=False,
    )
```

```python
import math

import jax
import jax.numpy as jnp
from jax import lax
from jax.experimental import pallas as pl
from jax.experimental.pallas import tpu as pltpu
from jax.sharding import PartitionSpec as P

MESH = pl.DeviceIdType.MESH
BACK = {"x": "x", "y": "y", "up": "down", "down": "up"}


def when(conds):
    conds = [c for c in conds if c is not None]
    if not conds:
        return lambda f: f()
    both = conds[0]
    for c in conds[1:]:
        both = jnp.logical_and(both, c)
    return pl.when(both)


class Grid:
    def __init__(self, n):
        self.n = n
        self.size = {"z": n // 4, "y": 2, "x": 2} if n % 4 == 0 else {"z": n, "y": 1, "x": 1}
        z = self.size["z"]
        self.rels = [
            (dz, fy, fx)
            for dz in range(1 - z, z)
            for fy in range(self.size["y"])
            for fx in range(self.size["x"])
        ]
        self.rels.sort(key=lambda r: (abs(r[0]) + r[1] + r[2], -abs(r[0])))

    def locate(self):
        me = lax.axis_index("row")
        ny, nx = self.size["y"], self.size["x"]
        self.me = me
        self.z = me // (ny * nx)
        self.y = (me // nx) % ny
        self.x = me % nx

    def coords(self, rel):
        dz, fy, fx = rel
        return {
            "z": self.z + dz,
            "y": 1 - self.y if fy else self.y,
            "x": 1 - self.x if fx else self.x,
        }

    def index(self, rel):
        c = self.coords(rel)
        return (c["z"] * self.size["y"] + c["y"]) * self.size["x"] + c["x"]

    def valid(self, rel):
        dz = rel[0]
        if dz == 0:
            return None
        return self.z < self.size["z"] - dz if dz > 0 else self.z >= -dz

    def neighbour(self, link):
        rel = {"x": (0, 0, 1), "y": (0, 1, 0), "up": (1, 0, 0), "down": (-1, 0, 0)}[link]
        return self.index(rel)

    def has(self, link):
        if link == "up":
            return self.z < self.size["z"] - 1
        if link == "down":
            return self.z > 0
        return None

    def links(self):
        found = [d for d in "xy" if self.size[d] > 1]
        return found + (["up", "down"] if self.size["z"] > 1 else [])

    def last(self, order, rel):
        differs = {"z": rel[0] != 0, "y": rel[1] != 0, "x": rel[2] != 0}
        found = [k for k, d in enumerate(order) if differs[d]]
        return found[-1] if found else -1

    def away(self, order, rel):
        k = self.last(order, rel)
        found = []
        for j, d in enumerate(order):
            if j < k or self.size[d] == 1:
                continue
            if d != "z":
                found += [d] if j > k else []
            elif j > k:
                found += ["up", "down"]
            else:
                found += ["down" if rel[0] > 0 else "up"]
        return found

    def towards(self, order, rel):
        d = order[self.last(order, rel)]
        if d != "z":
            return d
        return "up" if rel[0] > 0 else "down"

    def slot_dims(self, order, link):
        if link in "xy":
            return order[: order.index(link)]
        return order[: order.index("z") + 1]

    def slots(self, order, link):
        return math.prod(self.size[d] for d in self.slot_dims(order, link))

    def slot(self, order, link, rel):
        c = self.coords(rel)
        at = 0
        for d in self.slot_dims(order, link):
            at = at * self.size[d] + c[d]
        return at

    def barrier(self):
        barrier = pltpu.get_barrier_semaphore()
        count = 0
        for link in self.links():
            cond = self.has(link)

            @when([cond])
            def _(link=link):
                pl.semaphore_signal(
                    barrier, inc=1, device_id={"row": self.neighbour(link)}, device_id_type=MESH
                )

            count = count + (1 if cond is None else cond.astype(jnp.int32))
        pl.semaphore_wait(barrier, count)


def parts_of(width):
    tile = 128
    tiles = width // tile
    thin = tiles // 9
    if thin == 0:
        return [(0, width, "zyx")]
    wide = [(tiles - 2 * thin + 3 - i) // 4 for i in range(4)]
    pieces = [
        (wide[0], "zyx"),
        (wide[1], "zxy"),
        (thin, "xyz"),
        (thin, "yxz"),
        (wide[2], "zyx"),
        (wide[3], "zxy"),
    ]
    found, start = [], 0
    for count, order in pieces:
        if count:
            found.append((start * tile, count * tile, order))
            start += count
    return found


def sem_shapes(grid, orders):
    return [
        [pltpu.SemaphoreType.DMA((grid.slots(order, link),)) for link in grid.links()]
        for order in orders
    ]


def gather_start(grid, rel, part, order, src, dst, send, recv):
    row = grid.index(rel)
    for link in grid.away(order, rel):

        @when([grid.valid(rel), grid.has(link)])
        def _(link=link):
            gather_copy(grid, rel, part, order, link, src(row), dst(row), send, recv).start()


def gather_copy(grid, rel, part, order, link, src, dst, send, recv):
    return pltpu.make_async_remote_copy(
        src_ref=src,
        dst_ref=dst,
        send_sem=send[part][grid.links().index(link)].at[grid.slot(order, link, rel)],
        recv_sem=recv.at[part, grid.index(rel)],
        device_id={"row": grid.neighbour(link)},
        device_id_type=MESH,
    )


def gather_finish(grid, parts, dst, send, recv):
    for rel in grid.rels[1:]:
        for part, order in parts:

            @when([grid.valid(rel)])
            def _(rel=rel, part=part, order=order):
                row = grid.index(rel)
                pltpu.make_async_copy(dst(part, row), dst(part, row), recv.at[part, row]).wait()

            gather_start(
                grid, rel, part, order, lambda r: dst(part, r), lambda r: dst(part, r), send, recv
            )
    for rel in grid.rels:
        for part, order in parts:
            for link in grid.away(order, rel):

                @when([grid.valid(rel), grid.has(link)])
                def _(rel=rel, part=part, order=order, link=link):
                    ref = dst(part, grid.index(rel))
                    gather_copy(grid, rel, part, order, link, ref, ref, send, recv).wait_send()


def all_gather(block, collective_id):
    n = lax.axis_size("row")
    grid = Grid(n)
    parts = parts_of(block.shape[1]) if block.shape[1] >= 1152 else [(0, block.shape[1], "zyx")]
    numbered = [(i, order) for i, (_, _, order) in enumerate(parts)]

    def kernel(own, out, own_sem, recv, send):
        grid.locate()
        keep = pltpu.make_async_copy(own, out.at[grid.me], own_sem)
        keep.start()
        grid.barrier()

        def dst(part, row):
            start, width, _ = parts[part]
            return out.at[row, :, pl.ds(start, width)]

        for part, order in numbered:
            start, width, _ = parts[part]
            gather_start(
                grid,
                (0, 0, 0),
                part,
                order,
                lambda r: own.at[:, pl.ds(start, width)],
                lambda r: dst(part, r),
                send,
                recv,
            )
        gather_finish(grid, numbered, dst, send, recv)
        keep.wait()

    return pl.pallas_call(
        kernel,
        out_shape=jax.ShapeDtypeStruct((n, *block.shape), block.dtype),
        in_specs=[pl.BlockSpec(memory_space=pl.ANY)],
        out_specs=pl.BlockSpec(memory_space=pl.ANY),
        scratch_shapes=[
            pltpu.SemaphoreType.DMA,
            pltpu.SemaphoreType.DMA((len(parts), n)),
            sem_shapes(grid, [o for _, _, o in parts]),
        ],
        compiler_params=pltpu.CompilerParams(collective_id=collective_id, has_side_effects=True),
    )(block)


def tile_of(width, limit):
    return max([t for t in range(128, limit + 1, 128) if width % t == 0], default=width)


def all_reduce(arrays, collective_id):
    n = lax.axis_size("row")
    grid = Grid(n)
    parts = [(i, *p) for i, a in enumerate(arrays) for p in parts_of(a.shape[2])]
    parts.sort(key=lambda p: -p[0])
    orders = [p[3] for p in parts]
    numbered = list(enumerate(orders))
    count = len(arrays)

    def kernel(*refs):
        sources, outs, held = refs[:count], refs[count : 2 * count], refs[2 * count : 3 * count]
        inbox, load_sem, keep_sem, sum_send, sum_recv, send, recv = refs[3 * count :]
        grid.locate()

        def load(i, row):
            return pltpu.make_async_copy(sources[i].at[row], held[i].at[row], load_sem.at[i, row])

        for rel in reversed(grid.rels):
            for i in range(count):

                @when([grid.valid(rel)])
                def _(rel=rel, i=i):
                    load(i, grid.index(rel)).start()

        grid.barrier()

        def kept(part, row):
            i, start, width, _ = parts[part]
            return held[i].at[row, :, pl.ds(start, width)]

        def dst(part, row):
            i, start, width, _ = parts[part]
            return outs[i].at[row, :, pl.ds(start, width)]

        def sum_copy(rel, part, order):
            link = grid.towards(order, rel)
            at = grid.slot(order, BACK[link], rel)
            there = grid.links().index(BACK[link])
            row = grid.index(rel)
            return pltpu.make_async_remote_copy(
                src_ref=kept(part, row),
                dst_ref=inbox[part][there].at[at],
                send_sem=sum_send.at[part, row],
                recv_sem=sum_recv[part][there].at[at],
                device_id={"row": grid.neighbour(link)},
                device_id_type=MESH,
            )

        for rel in reversed(grid.rels):
            for i in range(count):

                @when([grid.valid(rel)])
                def _(rel=rel, i=i):
                    load(i, grid.index(rel)).wait()

            for part, order in numbered:
                i, start, width, _ = parts[part]
                for link in grid.away(order, rel):

                    @when([grid.valid(rel), grid.has(link)])
                    def _(rel=rel, part=part, order=order, link=link):
                        row, at = grid.index(rel), grid.slot(order, link, rel)
                        here = grid.links().index(link)
                        slot = inbox[part][here].at[at]
                        pltpu.make_async_copy(slot, slot, sum_recv[part][here].at[at]).wait()
                        columns = pl.ds(start, width)
                        held[i][row, :, columns] = held[i][row, :, columns] + inbox[part][here][at]

                if rel != (0, 0, 0):

                    @when([grid.valid(rel)])
                    def _(rel=rel, part=part, order=order):
                        sum_copy(rel, part, order).start()

                else:
                    pltpu.make_async_copy(
                        kept(part, grid.me), dst(part, grid.me), keep_sem.at[part]
                    ).start()
                    gather_start(
                        grid,
                        rel,
                        part,
                        order,
                        lambda r: kept(part, r),
                        lambda r: dst(part, r),
                        send,
                        recv,
                    )
        gather_finish(grid, numbered, dst, send, recv)
        for rel in grid.rels:
            for part, order in numbered:
                if rel != (0, 0, 0):

                    @when([grid.valid(rel)])
                    def _(rel=rel, part=part, order=order):
                        sum_copy(rel, part, order).wait_send()

                else:
                    pltpu.make_async_copy(
                        kept(part, grid.me), dst(part, grid.me), keep_sem.at[part]
                    ).wait()

    return pl.pallas_call(
        kernel,
        out_shape=[jax.ShapeDtypeStruct(a.shape, a.dtype) for a in arrays],
        in_specs=[pl.BlockSpec(memory_space=pl.ANY)] * count,
        out_specs=[pl.BlockSpec(memory_space=pl.ANY)] * count,
        scratch_shapes=[
            *[pltpu.VMEM(a.shape, a.dtype) for a in arrays],
            [
                [
                    pltpu.VMEM((grid.slots(order, link), arrays[i].shape[1], width), jnp.float32)
                    for link in grid.links()
                ]
                for i, _, width, order in parts
            ],
            pltpu.SemaphoreType.DMA((count, n)),
            pltpu.SemaphoreType.DMA((len(parts),)),
            pltpu.SemaphoreType.DMA((len(parts), n)),
            sem_shapes(grid, orders),
            sem_shapes(grid, orders),
            pltpu.SemaphoreType.DMA((len(parts), n)),
        ],
        compiler_params=pltpu.CompilerParams(
            collective_id=collective_id, has_side_effects=True, vmem_limit_bytes=60 * 2**20
        ),
    )(*arrays)


def deflate(kernel_rows, sums, rows, own):
    height, total = kernel_rows.shape
    comp = sums.shape[0]
    tile = tile_of(total, 2048)

    def body(kernel_ref, sums_ref, rows_ref, own_ref, deflated_ref, own_out):
        def times(left):
            return jnp.dot(
                left[...],
                sums_ref[...],
                precision=lax.Precision.HIGHEST,
                preferred_element_type=jnp.float32,
            )

        deflated_ref[...] = kernel_ref[...] - times(rows_ref)
        own_out[...] = times(own_ref)

    def columns(size):
        return pl.BlockSpec((size, tile), lambda i: (0, i))

    return pl.pallas_call(
        body,
        grid=(total // tile,),
        out_shape=[
            jax.ShapeDtypeStruct(kernel_rows.shape, jnp.float32),
            jax.ShapeDtypeStruct((own.shape[0], total), jnp.float32),
        ],
        in_specs=[
            columns(height),
            columns(comp),
            pl.BlockSpec(rows.shape, lambda i: (0, 0)),
            pl.BlockSpec(own.shape, lambda i: (0, 0)),
        ],
        out_specs=[columns(height), columns(own.shape[0])],
    )(kernel_rows, sums, rows, own)


def local(kernel, basis, responses):
    highest = lax.Precision.HIGHEST
    n = lax.axis_size("row")
    height, total = kernel.shape
    responses_here = responses.shape[1]
    row_count = height * n
    resp_count = responses_here * lax.axis_size("col")
    comp = basis.shape[1] * n
    root_rows = math.sqrt(row_count)
    last_dims = (((1,), (1,)), ((), ()))
    first_dims = (((0,), (0,)), ((), ()))

    all_basis = all_gather(basis.T, 0).reshape(comp, total)
    partial_proj = lax.dot_general(kernel, all_basis, last_dims, precision=highest)
    projected = lax.psum(partial_proj, "col")

    small_part = lax.dot_general(
        jnp.concatenate([responses, projected], axis=1), projected, first_dims, precision=highest
    )
    sums_part = lax.dot_general(projected, kernel, first_dims, precision=highest)
    sums, small = all_reduce(
        [
            sums_part.reshape(n, comp // n, total),
            small_part.reshape(n, (responses_here + comp) // n, comp),
        ],
        1,
    )
    small = small.reshape(responses_here + comp, comp)
    factor = jnp.linalg.cholesky(small[responses_here:] / row_count)
    right = jnp.concatenate(
        [projected.T, small[:responses_here].T, jnp.eye(comp, dtype=jnp.float32)], axis=1
    )
    solved = jax.scipy.linalg.solve_triangular(factor, right, lower=True)
    scores = solved[:, :height].T
    weights = solved[:, height : height + responses_here].T / root_rows
    inverse = solved[:, height + responses_here :] / root_rows
    next_part = jnp.dot(responses, weights, precision=highest) / math.sqrt(resp_count)
    basis_next = lax.psum(next_part, "col")
    deflated, loadings = deflate(
        kernel,
        sums.reshape(comp, total),
        jnp.dot(scores, inverse, precision=highest) / root_rows,
        lax.dynamic_slice_in_dim(inverse, lax.axis_index("row") * (comp // n), comp // n),
    )
    return (scores, loadings, weights, deflated, basis_next)


def solution(mesh):
    return jax.shard_map(
        local,
        mesh=mesh,
        in_specs=(P("row", "col"), P("col", "row"), P("row", "col")),
        out_specs=(
            P("row", None),
            P("row", "col"),
            P("col", None),
            P("row", "col"),
            P("row", None),
        ),
        check_vma=False,
    )
```

```python
import math

import jax
import jax.numpy as jnp
from jax import lax
from jax.experimental import pallas as pl
from jax.experimental.pallas import tpu as pltpu
from jax.sharding import PartitionSpec as P

MESH = pl.DeviceIdType.MESH
BACK = {"x": "x", "y": "y", "up": "down", "down": "up"}


def when(conds):
    conds = [c for c in conds if c is not None]
    if not conds:
        return lambda f: f()
    both = conds[0]
    for c in conds[1:]:
        both = jnp.logical_and(both, c)
    return pl.when(both)


class Grid:
    def __init__(self, n):
        self.n = n
        self.size = {"z": n // 4, "y": 2, "x": 2} if n % 4 == 0 else {"z": n, "y": 1, "x": 1}
        z = self.size["z"]
        self.rels = [
            (dz, fy, fx)
            for dz in range(1 - z, z)
            for fy in range(self.size["y"])
            for fx in range(self.size["x"])
        ]
        self.rels.sort(key=lambda r: (abs(r[0]) + r[1] + r[2], -abs(r[0])))

    def locate(self):
        me = lax.axis_index("row")
        ny, nx = self.size["y"], self.size["x"]
        self.me = me
        self.z = me // (ny * nx)
        self.y = (me // nx) % ny
        self.x = me % nx

    def coords(self, rel):
        dz, fy, fx = rel
        return {
            "z": self.z + dz,
            "y": 1 - self.y if fy else self.y,
            "x": 1 - self.x if fx else self.x,
        }

    def index(self, rel):
        c = self.coords(rel)
        return (c["z"] * self.size["y"] + c["y"]) * self.size["x"] + c["x"]

    def valid(self, rel):
        dz = rel[0]
        if dz == 0:
            return None
        return self.z < self.size["z"] - dz if dz > 0 else self.z >= -dz

    def neighbour(self, link):
        rel = {"x": (0, 0, 1), "y": (0, 1, 0), "up": (1, 0, 0), "down": (-1, 0, 0)}[link]
        return self.index(rel)

    def has(self, link):
        if link == "up":
            return self.z < self.size["z"] - 1
        if link == "down":
            return self.z > 0
        return None

    def links(self):
        found = [d for d in "xy" if self.size[d] > 1]
        return found + (["up", "down"] if self.size["z"] > 1 else [])

    def last(self, order, rel):
        differs = {"z": rel[0] != 0, "y": rel[1] != 0, "x": rel[2] != 0}
        found = [k for k, d in enumerate(order) if differs[d]]
        return found[-1] if found else -1

    def away(self, order, rel):
        k = self.last(order, rel)
        found = []
        for j, d in enumerate(order):
            if j < k or self.size[d] == 1:
                continue
            if d != "z":
                found += [d] if j > k else []
            elif j > k:
                found += ["up", "down"]
            else:
                found += ["down" if rel[0] > 0 else "up"]
        return found

    def towards(self, order, rel):
        d = order[self.last(order, rel)]
        if d != "z":
            return d
        return "up" if rel[0] > 0 else "down"

    def slot_dims(self, order, link):
        if link in "xy":
            return order[: order.index(link)]
        return order[: order.index("z") + 1]

    def slots(self, order, link):
        return math.prod(self.size[d] for d in self.slot_dims(order, link))

    def slot(self, order, link, rel):
        c = self.coords(rel)
        at = 0
        for d in self.slot_dims(order, link):
            at = at * self.size[d] + c[d]
        return at

    def barrier(self):
        barrier = pltpu.get_barrier_semaphore()
        count = 0
        for link in self.links():
            cond = self.has(link)

            @when([cond])
            def _(link=link):
                pl.semaphore_signal(
                    barrier, inc=1, device_id={"row": self.neighbour(link)}, device_id_type=MESH
                )

            count = count + (1 if cond is None else cond.astype(jnp.int32))
        pl.semaphore_wait(barrier, count)


def parts_of(width):
    tile = 128
    tiles = width // tile
    thin = tiles // 9
    if thin == 0:
        return [(0, width, "zyx")]
    wide = [(tiles - 2 * thin + 3 - i) // 4 for i in range(4)]
    pieces = [
        (wide[0], "zyx"),
        (wide[1], "zxy"),
        (thin, "xyz"),
        (thin, "yxz"),
        (wide[2], "zyx"),
        (wide[3], "zxy"),
    ]
    found, start = [], 0
    for count, order in pieces:
        if count:
            found.append((start * tile, count * tile, order))
            start += count
    return found


def sem_shapes(grid, orders):
    return [
        [pltpu.SemaphoreType.DMA((grid.slots(order, link),)) for link in grid.links()]
        for order in orders
    ]


def gather_start(grid, rel, part, order, src, dst, send, recv):
    row = grid.index(rel)
    for link in grid.away(order, rel):

        @when([grid.valid(rel), grid.has(link)])
        def _(link=link):
            gather_copy(grid, rel, part, order, link, src(row), dst(row), send, recv).start()


def gather_copy(grid, rel, part, order, link, src, dst, send, recv):
    return pltpu.make_async_remote_copy(
        src_ref=src,
        dst_ref=dst,
        send_sem=send[part][grid.links().index(link)].at[grid.slot(order, link, rel)],
        recv_sem=recv.at[part, grid.index(rel)],
        device_id={"row": grid.neighbour(link)},
        device_id_type=MESH,
    )


def gather_finish(grid, parts, dst, send, recv):
    for rel in grid.rels[1:]:
        for part, order in parts:

            @when([grid.valid(rel)])
            def _(rel=rel, part=part, order=order):
                row = grid.index(rel)
                pltpu.make_async_copy(dst(part, row), dst(part, row), recv.at[part, row]).wait()

            gather_start(
                grid, rel, part, order, lambda r: dst(part, r), lambda r: dst(part, r), send, recv
            )
    for rel in grid.rels:
        for part, order in parts:
            for link in grid.away(order, rel):

                @when([grid.valid(rel), grid.has(link)])
                def _(rel=rel, part=part, order=order, link=link):
                    ref = dst(part, grid.index(rel))
                    gather_copy(grid, rel, part, order, link, ref, ref, send, recv).wait_send()


def all_gather(block, collective_id):
    n = lax.axis_size("row")
    grid = Grid(n)
    parts = parts_of(block.shape[1]) if block.shape[1] >= 1152 else [(0, block.shape[1], "zyx")]
    numbered = [(i, order) for i, (_, _, order) in enumerate(parts)]

    def kernel(own, out, own_sem, recv, send):
        grid.locate()
        keep = pltpu.make_async_copy(own, out.at[grid.me], own_sem)
        keep.start()
        grid.barrier()

        def dst(part, row):
            start, width, _ = parts[part]
            return out.at[row, :, pl.ds(start, width)]

        for part, order in numbered:
            start, width, _ = parts[part]
            gather_start(
                grid,
                (0, 0, 0),
                part,
                order,
                lambda r: own.at[:, pl.ds(start, width)],
                lambda r: dst(part, r),
                send,
                recv,
            )
        gather_finish(grid, numbered, dst, send, recv)
        keep.wait()

    return pl.pallas_call(
        kernel,
        out_shape=jax.ShapeDtypeStruct((n, *block.shape), block.dtype),
        in_specs=[pl.BlockSpec(memory_space=pl.ANY)],
        out_specs=pl.BlockSpec(memory_space=pl.ANY),
        scratch_shapes=[
            pltpu.SemaphoreType.DMA,
            pltpu.SemaphoreType.DMA((len(parts), n)),
            sem_shapes(grid, [o for _, _, o in parts]),
        ],
        compiler_params=pltpu.CompilerParams(collective_id=collective_id, has_side_effects=True),
    )(block)


def tile_of(width, limit):
    return max([t for t in range(128, limit + 1, 128) if width % t == 0], default=width)


def all_reduce(arrays, collective_id):
    n = lax.axis_size("row")
    grid = Grid(n)
    parts = [(i, *p) for i, a in enumerate(arrays) for p in parts_of(a.shape[2])]
    parts.sort(key=lambda p: -p[0])
    orders = [p[3] for p in parts]
    numbered = list(enumerate(orders))
    count = len(arrays)

    def kernel(*refs):
        sources, outs, held = refs[:count], refs[count : 2 * count], refs[2 * count : 3 * count]
        inbox, load_sem, keep_sem, sum_send, sum_recv, send, recv = refs[3 * count :]
        grid.locate()

        def load(i, row):
            return pltpu.make_async_copy(sources[i].at[row], held[i].at[row], load_sem.at[i, row])

        for rel in reversed(grid.rels):
            for i in range(count):

                @when([grid.valid(rel)])
                def _(rel=rel, i=i):
                    load(i, grid.index(rel)).start()

        grid.barrier()

        def kept(part, row):
            i, start, width, _ = parts[part]
            return held[i].at[row, :, pl.ds(start, width)]

        def dst(part, row):
            i, start, width, _ = parts[part]
            return outs[i].at[row, :, pl.ds(start, width)]

        def sum_copy(rel, part, order):
            link = grid.towards(order, rel)
            at = grid.slot(order, BACK[link], rel)
            there = grid.links().index(BACK[link])
            row = grid.index(rel)
            return pltpu.make_async_remote_copy(
                src_ref=kept(part, row),
                dst_ref=inbox[part][there].at[at],
                send_sem=sum_send.at[part, row],
                recv_sem=sum_recv[part][there].at[at],
                device_id={"row": grid.neighbour(link)},
                device_id_type=MESH,
            )

        for rel in reversed(grid.rels):
            for i in range(count):

                @when([grid.valid(rel)])
                def _(rel=rel, i=i):
                    load(i, grid.index(rel)).wait()

            for part, order in numbered:
                i, start, width, _ = parts[part]
                for link in grid.away(order, rel):

                    @when([grid.valid(rel), grid.has(link)])
                    def _(rel=rel, part=part, order=order, link=link):
                        row, at = grid.index(rel), grid.slot(order, link, rel)
                        here = grid.links().index(link)
                        slot = inbox[part][here].at[at]
                        pltpu.make_async_copy(slot, slot, sum_recv[part][here].at[at]).wait()
                        columns = pl.ds(start, width)
                        held[i][row, :, columns] = held[i][row, :, columns] + inbox[part][here][at]

                if rel != (0, 0, 0):

                    @when([grid.valid(rel)])
                    def _(rel=rel, part=part, order=order):
                        sum_copy(rel, part, order).start()

                else:
                    pltpu.make_async_copy(
                        kept(part, grid.me), dst(part, grid.me), keep_sem.at[part]
                    ).start()
                    gather_start(
                        grid,
                        rel,
                        part,
                        order,
                        lambda r: kept(part, r),
                        lambda r: dst(part, r),
                        send,
                        recv,
                    )
        gather_finish(grid, numbered, dst, send, recv)
        for rel in grid.rels:
            for part, order in numbered:
                if rel != (0, 0, 0):

                    @when([grid.valid(rel)])
                    def _(rel=rel, part=part, order=order):
                        sum_copy(rel, part, order).wait_send()

                else:
                    pltpu.make_async_copy(
                        kept(part, grid.me), dst(part, grid.me), keep_sem.at[part]
                    ).wait()

    return pl.pallas_call(
        kernel,
        out_shape=[jax.ShapeDtypeStruct(a.shape, a.dtype) for a in arrays],
        in_specs=[pl.BlockSpec(memory_space=pl.ANY)] * count,
        out_specs=[pl.BlockSpec(memory_space=pl.ANY)] * count,
        scratch_shapes=[
            *[pltpu.VMEM(a.shape, a.dtype) for a in arrays],
            [
                [
                    pltpu.VMEM((grid.slots(order, link), arrays[i].shape[1], width), jnp.float32)
                    for link in grid.links()
                ]
                for i, _, width, order in parts
            ],
            pltpu.SemaphoreType.DMA((count, n)),
            pltpu.SemaphoreType.DMA((len(parts),)),
            pltpu.SemaphoreType.DMA((len(parts), n)),
            sem_shapes(grid, orders),
            sem_shapes(grid, orders),
            pltpu.SemaphoreType.DMA((len(parts), n)),
        ],
        compiler_params=pltpu.CompilerParams(
            collective_id=collective_id, has_side_effects=True, vmem_limit_bytes=60 * 2**20
        ),
    )(*arrays)


def deflate(kernel_rows, sums, rows, own):
    height, total = kernel_rows.shape
    comp = sums.shape[0]
    tile = tile_of(total, 2048)

    def body(kernel_ref, sums_ref, rows_ref, own_ref, deflated_ref, own_out):
        both = jnp.concatenate([rows_ref[...], own_ref[...]], axis=0)
        product = jnp.dot(
            both,
            sums_ref[...],
            precision=lax.Precision.HIGHEST,
            preferred_element_type=jnp.float32,
        )
        deflated_ref[...] = kernel_ref[...] - product[:height]
        own_out[...] = product[height:]

    def columns(size):
        return pl.BlockSpec((size, tile), lambda i: (0, i))

    return pl.pallas_call(
        body,
        grid=(total // tile,),
        out_shape=[
            jax.ShapeDtypeStruct(kernel_rows.shape, jnp.float32),
            jax.ShapeDtypeStruct((own.shape[0], total), jnp.float32),
        ],
        in_specs=[
            columns(height),
            columns(comp),
            pl.BlockSpec(rows.shape, lambda i: (0, 0)),
            pl.BlockSpec(own.shape, lambda i: (0, 0)),
        ],
        out_specs=[columns(height), columns(own.shape[0])],
    )(kernel_rows, sums, rows, own)


def local(kernel, basis, responses):
    highest = lax.Precision.HIGHEST
    n = lax.axis_size("row")
    height, total = kernel.shape
    responses_here = responses.shape[1]
    row_count = height * n
    resp_count = responses_here * lax.axis_size("col")
    comp = basis.shape[1] * n
    root_rows = math.sqrt(row_count)
    last_dims = (((1,), (1,)), ((), ()))
    first_dims = (((0,), (0,)), ((), ()))

    all_basis = all_gather(basis.T, 0).reshape(comp, total)
    partial_proj = lax.dot_general(kernel, all_basis, last_dims, precision=highest)
    projected = lax.psum(partial_proj, "col")

    small_part = lax.dot_general(
        jnp.concatenate([responses, projected], axis=1), projected, first_dims, precision=highest
    )
    sums_part = lax.dot_general(projected, kernel, first_dims, precision=highest)
    sums, small = all_reduce(
        [
            sums_part.reshape(n, comp // n, total),
            small_part.reshape(n, (responses_here + comp) // n, comp),
        ],
        1,
    )
    small = small.reshape(responses_here + comp, comp)
    factor = jnp.linalg.cholesky(small[responses_here:] / row_count)
    right = jnp.concatenate(
        [projected.T, small[:responses_here].T, jnp.eye(comp, dtype=jnp.float32)], axis=1
    )
    solved = jax.scipy.linalg.solve_triangular(factor, right, lower=True)
    scores = solved[:, :height].T
    weights = solved[:, height : height + responses_here].T / root_rows
    inverse = solved[:, height + responses_here :] / root_rows
    next_part = jnp.dot(responses, weights, precision=highest) / math.sqrt(resp_count)
    basis_next = lax.psum(next_part, "col")
    deflated, loadings = deflate(
        kernel,
        sums.reshape(comp, total),
        jnp.dot(scores, inverse, precision=highest) / root_rows,
        lax.dynamic_slice_in_dim(inverse, lax.axis_index("row") * (comp // n), comp // n),
    )
    return (scores, loadings, weights, deflated, basis_next)


def solution(mesh):
    return jax.shard_map(
        local,
        mesh=mesh,
        in_specs=(P("row", "col"), P("col", "row"), P("row", "col")),
        out_specs=(
            P("row", None),
            P("row", "col"),
            P("col", None),
            P("row", "col"),
            P("row", None),
        ),
        check_vma=False,
    )
```
